512 devices in a mesh: branch: 2 (over z_hi), row: 16 (over z_lo, core), col: 16 (over y, x).
Axes of the slice: x: 4, y: 4, z: 16 (z_hi: 2, z_lo: 8; z = z_hi * 8 + z_lo), core: 2. Of those that a mesh axis runs over, the one named last changes fastest.
Arguments:
- pool_inverse: float32 [4096, 4096], P('row', 'col'), as said below
- ancestors: int32 [2, 2, 64], P('branch'), may hold values from 0 to 64, as said below
- panel_one: float32 [2, 4096, 1024], P('branch', 'row', 'col'), may hold values from -0.09375 to 0.09375
- diag_one: float32 [2, 1024, 1024], P('branch', 'row', 'col')
- panel_two: float32 [2, 4096, 1024], P('branch', 'row', 'col'), may hold values from -0.09375 to 0.09375
- coupling: float32 [2, 1024, 1024], P('branch', 'row', 'col'), may hold values from -0.1875 to 0.1875
- diag_two: float32 [2, 1024, 1024], P('branch', 'row', 'col')
Outputs:
- parent_column: float32 [2, 4096, 1024], P('branch', 'row', 'col')
- parent_diagonal: float32 [2, 1024, 1024], P('branch', 'row', 'col')
- child_column: float32 [2, 4096, 1024], P('branch', 'row', 'col')
- child_coupling: float32 [2, 1024, 1024], P('branch', 'row', 'col')
- child_diagonal: float32 [2, 1024, 1024], P('branch', 'row', 'col')
The draws below stay inside these ranges and needn't reach their ends.
Inputs may be any that keep to these rules, and one draw needn't show every extreme that they name: pool_inverse is symmetric. `ancestors`: for each subtree and level the live entries are distinct pool block numbers in increasing order, followed by entries equal to 64; a subtree's level-two live blocks are among its level-one live blocks; each range of 4 blocks starting at a multiple of 4 holds at least one level-two live block.
All inputs are finite; a program needn't handle non-finite values.
Results may differ from the reference program's by a relative error of at most 0.0001.
Values sent between devices are 32-bit elements; how exact they have to be, the bound alone decides.
No kernel may reach another device: no remote copies, remote signals or barrier semaphores. Data moves between devices by JAX's collectives and lax.ppermute only.
A program may use at most 64 MiB of HBM per device.

```python
import math
import jax
import jax.numpy as jnp
from jax import lax

W = 1024
RB = 64
PB_DEV = 4
PB = 64
POOL = 4096
BRANCHES = 2


def draw_pool_inverse(key, part):
    key_off = jax.random.fold_in(key, 11)
    key_diag = jax.random.fold_in(key, 12)
    normals = jax.random.normal(key_off, (POOL, POOL), jnp.float32)
    offdiag = (normals + normals.T) * (4.0 / math.sqrt(2.0 * POOL))
    diagonal = jax.random.uniform(key_diag, (POOL,), jnp.float32, 10.0, 22.0)
    matrix = offdiag + jnp.diag(diagonal)
    return matrix


def spd_blocks(key, low, high):
    key_off = jax.random.fold_in(key, 21)
    key_diag = jax.random.fold_in(key, 22)
    normals = jax.random.normal(key_off, (BRANCHES, W, W), jnp.float32)
    offdiag = (normals + jnp.swapaxes(normals, 1, 2)) * (0.05 / math.sqrt(2.0))
    diagonal = jax.random.uniform(key_diag, (BRANCHES, W), jnp.float32, low, high)
    return offdiag + diagonal[:, :, None] * jnp.eye(W, dtype=jnp.float32)[None]


def draw_diag_one(key, part):
    base = jax.random.fold_in(key, 31)
    return spd_blocks(base, 3.0, 8.0)


def draw_diag_two(key, part):
    base = jax.random.fold_in(key, 41)
    return spd_blocks(base, 3.0, 8.0)


def draw_ancestors(key, part):
    segments = PB // PB_DEV
    key_rate = jax.random.fold_in(key, 51)
    key_bits = jax.random.fold_in(key, 52)
    key_force = jax.random.fold_in(key, 53)
    key_keep = jax.random.fold_in(key, 54)
    rates = jax.random.randint(key_rate, (BRANCHES, segments), 1, 5)
    bits = jax.random.randint(key_bits, (BRANCHES, PB), 0, 4)
    live_one = bits < jnp.repeat(rates, PB_DEV, axis=1)
    forced_at = jax.random.randint(key_force, (BRANCHES, segments), 0, PB_DEV)
    forced = (jnp.arange(PB_DEV)[None, None, :] == forced_at[:, :, None]).reshape(BRANCHES, PB)
    keeping = jax.random.randint(key_keep, (BRANCHES, PB), 0, 2) == 1
    live_one = live_one | forced
    live_two = live_one & keeping | forced
    numbers = jnp.arange(PB, dtype=jnp.int32)[None, :]
    listed_one = jnp.sort(jnp.where(live_one, numbers, PB), axis=1)
    listed_two = jnp.sort(jnp.where(live_two, numbers, PB), axis=1)
    return jnp.stack([listed_one, listed_two], axis=1).astype(jnp.int32)


def steps_of(key, shape, cuts, smallest, high):
    def one(axis_at, parts):
        draws = jax.random.uniform(jax.random.fold_in(jax.random.fold_in(key, 6), axis_at), (parts,), jnp.float32, smallest / len(cuts), high / len(cuts))
        return jnp.repeat(jnp.exp(draws), shape[axis_at] // parts).reshape((-1,) + (1,) * (len(shape) - axis_at - 1))

    level = one(*cuts[0])
    for cut in cuts[1:]:
        level = level * one(*cut)
    return level


def bell_draw(key, shape, width, most, split=(), kind=jnp.bfloat16):
    entries = jax.random.normal(key, shape, jnp.float32) * width
    if len(split) > 0:
        entries = steps_of(key, shape, split, -0.22, 0.18) * entries
    return jnp.clip(entries, min=-most, max=most).astype(kind)


def setup_inputs(seed: int = 0) -> dict:
    streams_of = jax.random.split(jax.random.key(seed), 8)
    return {
        "pool_inverse": draw_pool_inverse(jax.random.fold_in(streams_of[7], 71), 0),
        "ancestors": draw_ancestors(jax.random.fold_in(streams_of[7], 71), 0),
        "panel_one": bell_draw(streams_of[2], (BRANCHES, POOL, W), POOL ** -0.5, 0.09375, ((0, 2), (1, 16), (2, 16)), jnp.float32),
        "diag_one": draw_diag_one(jax.random.fold_in(streams_of[7], 71), 0),
        "panel_two": bell_draw(streams_of[4], (BRANCHES, POOL, W), POOL ** -0.5, 0.09375, ((0, 2), (1, 16), (2, 16)), jnp.float32),
        "coupling": bell_draw(streams_of[5], (BRANCHES, W, W), W ** -0.5, 0.1875, ((0, 2), (1, 16), (2, 16)), jnp.float32),
        "diag_two": draw_diag_two(jax.random.fold_in(streams_of[7], 71), 0),
    }


def matmul(left, right):
    return jnp.dot(left, right, precision=lax.Precision.HIGHEST, preferred_element_type=jnp.float32)


def inner_product(left, right):
    return lax.dot_general(left, right, (((0,), (0,)), ((), ())), precision=lax.Precision.HIGHEST, preferred_element_type=jnp.float32)


def live_rows(listing):
    blocks = jnp.arange(PB, dtype=jnp.int32)
    is_live = jnp.any(blocks[:, None] == listing[None, :].astype(jnp.int32), axis=1)
    return jnp.repeat(is_live.astype(jnp.float32), RB)[:, None]


def reference(pool_inverse, ancestors, panel_one, diag_one, panel_two, coupling, diag_two):
    parents, parent_diags, childs, couplings, child_diags = [], [], [], [], []
    for member in range(BRANCHES):
        mask_one = live_rows(ancestors[member, 0])
        mask_two = live_rows(ancestors[member, 1])
        lower_one = panel_one[member] * mask_one
        lower_two = panel_two[member] * mask_two
        link_block = coupling[member]
        parent_block = -matmul(pool_inverse, lower_one)
        parent_diag = diag_one[member] - inner_product(lower_one, parent_block)
        child_block = -(matmul(parent_block, link_block) + matmul(pool_inverse, lower_two))
        coupled = -(matmul(parent_diag, link_block) + inner_product(parent_block, lower_two))
        child_diag = diag_two[member] - inner_product(link_block, coupled) - inner_product(lower_two, child_block)
        parents.append(parent_block * mask_one)
        parent_diags.append(parent_diag)
        childs.append(child_block * mask_two)
        couplings.append(coupled)
        child_diags.append(child_diag)
    return (jnp.stack(parents), jnp.stack(parent_diags), jnp.stack(childs), jnp.stack(couplings), jnp.stack(child_diags))
```

```python
import jax
import jax.numpy as jnp
from jax import lax
from jax.sharding import PartitionSpec as P

RB = 64
COLS = 16
QUADS = [[h * 8 + q * 2 + s for q in range(4)] for h in range(2) for s in range(2)]


def dot(left, right, contract):
    return lax.dot_general(
        left,
        right,
        (contract, ((), ())),
        precision=lax.Precision.HIGH,
        preferred_element_type=jnp.float32,
    )


def swap(value, bit):
    return lax.ppermute(value, "row", [(i, i ^ bit) for i in range(16)])


def gather_cols(value):
    return lax.all_to_all(jnp.broadcast_to(value[None], (COLS,) + value.shape), "col", 0, 0)


def gather_rows(value, row_index):
    lead = 0
    for bit in (8, 4, 2, 1):
        other = swap(value, bit)
        low = (row_index & bit) == 0
        value = jnp.stack([jnp.where(low, value, other), jnp.where(low, other, value)], axis=lead)
        lead += 1
    return value.reshape((16,) + value.shape[4:])


def crossed(value, flip):
    return lax.ppermute(
        value, ("row", "col"), [(r * 16 + c, c * 16 + (r ^ flip)) for r in range(16) for c in range(16)]
    )


def shards(pool_inverse, ancestors, panel_one, diag_one, panel_two, coupling, diag_two):
    rows = pool_inverse.shape[0]
    width = panel_one.shape[2]
    side = diag_one.shape[1]
    row_index = lax.axis_index("row")
    blocks_here = rows // RB
    core = row_index & 1
    far = (row_index >> 3) & 1
    own_blocks = row_index * blocks_here + jnp.arange(blocks_here, dtype=jnp.int32)

    def live_rows(listing):
        is_live = jnp.any(own_blocks[:, None] == listing[None, :], axis=1)
        return jnp.repeat(is_live.astype(jnp.float32), RB)[None, :]

    mask_one = live_rows(ancestors[0, 0])
    mask_two = live_rows(ancestors[0, 1])
    one_t = panel_one[0].T * mask_one
    two_t = panel_two[0].T * mask_two
    link = coupling[0]

    packed = jnp.concatenate([one_t, diag_one[0].T, link.T], axis=1)
    gathered = gather_cols(packed).reshape(COLS * width, rows + 2 * side)
    link_col = gather_rows(link, row_index).reshape(16 * side, width)

    product = dot(link_col, gathered[:, : rows + side], ((0,), (0,)))
    k_t = product[:, :rows] - two_t
    dc_t = product[:, rows:]

    one_all = gathered[:, :rows].reshape(8, 2, width, rows)
    link_all = gathered[:, rows + side :]
    k_all = gather_cols(k_t).reshape(8, 2, width, rows)

    both = jnp.stack([one_all, k_all])

    def term(which):
        part = lax.dynamic_index_in_dim(both, which, axis=2, keepdims=False)
        out = dot(part.reshape(2 * 8 * width, rows), pool_inverse, ((1,), (0,)))
        return out.reshape(2, 2, 4, width, rows)

    arrived = swap(term(1 - core), 1)
    summed = term(core) + arrived
    quad = lax.all_to_all(jnp.moveaxis(summed, 2, 0), "row", 0, 0, axis_index_groups=QUADS)
    quad = jnp.sum(quad, axis=0)
    near_block = lax.dynamic_index_in_dim(quad, far, axis=1, keepdims=False)
    far_block = lax.dynamic_index_in_dim(quad, 1 - far, axis=1, keepdims=False)
    value = crossed(near_block, 0) + crossed(far_block, 8)
    v_t, y_t = value[0], value[1]

    one_y = dot(one_all.reshape(-1, rows), value.reshape(2 * width, rows), ((1,), (1,)))
    k_flat = k_all.reshape(-1, rows)
    k_y = dot(k_flat, y_t, ((1,), (1,))) + dot(link_all, dc_t, ((1,), (1,)))
    k_y = k_y.reshape(2, 4, 2, side, width)
    one_y = one_y.reshape(2, 4, 2, side, 2 * width)
    final = jnp.concatenate(
        [one_y[0], one_y[1], jnp.concatenate([k_y[0], k_y[1]], axis=-1)], axis=2
    )
    arrived = swap(lax.dynamic_index_in_dim(final, 1 - core, axis=1, keepdims=False), 1)
    final = lax.dynamic_index_in_dim(final, core, axis=1, keepdims=False) + arrived
    final = jnp.sum(lax.all_to_all(final, "row", 0, 0, axis_index_groups=QUADS), axis=0)
    pz = final[: 2 * side].reshape(2, side, 2 * width)
    ss = final[2 * side :]
    keep = lax.dynamic_index_in_dim(pz, far, axis=0, keepdims=False)
    give = lax.dynamic_index_in_dim(pz, 1 - far, axis=0, keepdims=False)
    arrived = swap(jnp.concatenate([give, ss], axis=0), 8)
    keep = keep + arrived[:side]
    ss = ss + arrived[side:]
    ss = jnp.where(far == 0, ss[:, :width], ss[:, width:])

    parent_diag = diag_one[0] + keep[:, :width]
    coupled = -(dc_t.T + keep[:, width:])
    child_diag = diag_two[0] + ss
    return (
        -(v_t * mask_one).T[None],
        parent_diag[None],
        (y_t * mask_two).T[None],
        coupled[None],
        child_diag[None],
    )


def solution(mesh):
    placed = (
        P("row", "col"),
        P("branch", None, None),
        P("branch", "row", "col"),
        P("branch", "row", "col"),
        P("branch", "row", "col"),
        P("branch", "row", "col"),
        P("branch", "row", "col"),
    )
    return jax.shard_map(
        shards,
        mesh=mesh,
        in_specs=placed,
        out_specs=(P("branch", "row", "col"),) * 5,
        check_vma=False,
    )
```

```python
import jax
import jax.numpy as jnp
from jax import lax
from jax.sharding import PartitionSpec as P


RB = 64
COLS = 16
QUADS = [[h * 8 + q * 2 + s for q in range(4)] for h in range(2) for s in range(2)]


def dot(left, right, contract):
    return lax.dot_general(
        left,
        right,
        (contract, ((), ())),
        precision=lax.Precision.HIGH,
        preferred_element_type=jnp.float32,
    )


def swap(value, bit):
    return lax.ppermute(value, "row", [(i, i ^ bit) for i in range(16)])


def gather_cols(value):
    return lax.all_to_all(jnp.broadcast_to(value[None], (COLS,) + value.shape), "col", 0, 0)


def gather_rows(value, row_index):
    lead = 0
    for bit in (8, 4, 2, 1):
        other = swap(value, bit)
        low = (row_index & bit) == 0
        value = jnp.stack([jnp.where(low, value, other), jnp.where(low, other, value)], axis=lead)
        lead += 1
    return value.reshape((16,) + value.shape[4:])


def crossed(value, flip):
    return lax.ppermute(
        value, ("row", "col"), [(r * 16 + c, c * 16 + (r ^ c ^ flip)) for r in range(16) for c in range(16)]
    )


def body(pool_inverse, ancestors, panel_one, diag_one, panel_two, coupling, diag_two):
    rows = pool_inverse.shape[0]
    width = panel_one.shape[2]
    side = diag_one.shape[1]
    row_index = lax.axis_index("row")
    blocks_here = rows // RB
    core = row_index & 1
    far = (row_index >> 3) & 1
    own_blocks = row_index * blocks_here + jnp.arange(blocks_here, dtype=jnp.int32)

    def live_rows(listing):
        is_live = jnp.any(own_blocks[:, None] == listing[None, :], axis=1)
        return jnp.repeat(is_live.astype(jnp.float32), RB)[None, :]

    mask_one = live_rows(ancestors[0, 0])
    mask_two = live_rows(ancestors[0, 1])
    one_t = panel_one[0].T * mask_one
    two_t = panel_two[0].T * mask_two
    link = coupling[0]

    gathered = gather_cols(one_t)
    link_col = gather_rows(link, row_index).reshape(16 * side, width)
    one_flat = gathered.reshape(COLS * width, rows)
    k_t = dot(link_col, one_flat, ((0,), (0,))) - two_t
    k_all = gather_cols(k_t)

    def pick(value, index, axis):
        return lax.dynamic_index_in_dim(value, index, axis=axis, keepdims=False)

    slot = row_index ^ lax.axis_index("col")
    core_bit, q0, q1, far_bit = slot & 1, (slot >> 1) & 1, (slot >> 2) & 1, (slot >> 3) & 1

    def term(blocks, which):
        part = pick(blocks.reshape(8, 2, width, rows), which, 1)
        out = dot(part.reshape(8 * width, rows), pool_inverse, ((1,), (0,)))
        return out.reshape(2, 2, 2, width, rows)

    def row_sum(blocks):
        total = term(blocks, core_bit) + swap(term(blocks, 1 - core_bit), 1)
        total = pick(total, q0, 2) + swap(pick(total, 1 - q0, 2), 2)
        return pick(total, q1, 1) + swap(pick(total, 1 - q1, 1), 4)

    def cross(total):
        own = crossed(pick(total, far_bit, 0), 0)
        return own + crossed(pick(total, 1 - far_bit, 0), 8)

    early, _ = lax.optimization_barrier((gathered, k_t))
    v_sum = row_sum(early)
    k_all, v_sum = lax.optimization_barrier((k_all, v_sum))
    v_t = cross(v_sum)
    y_sum = row_sum(k_all)
    y_t = cross(y_sum)

    packed = jnp.concatenate([diag_one[0].T, link.T], axis=1)
    packed, _ = lax.optimization_barrier((packed, y_sum))
    packed = gather_cols(packed).reshape(COLS * width, 2 * side)
    dc_t = dot(link_col, packed[:, :side], ((0,), (0,)))
    link_all = packed[:, side:]
    value = jnp.concatenate([v_t, y_t], axis=0)

    one_y = dot(one_flat, value, ((1,), (1,)))
    k_flat = k_all.reshape(-1, rows)
    k_y = dot(k_flat, y_t, ((1,), (1,))) + dot(link_all, dc_t, ((1,), (1,)))
    k_y = k_y.reshape(2, 4, 2, side, width)
    one_y = one_y.reshape(2, 4, 2, side, 2 * width)
    final = jnp.concatenate(
        [one_y[0], one_y[1], jnp.concatenate([k_y[0], k_y[1]], axis=-1)], axis=2
    )
    arrived = swap(lax.dynamic_index_in_dim(final, 1 - core, axis=1, keepdims=False), 1)
    final = lax.dynamic_index_in_dim(final, core, axis=1, keepdims=False) + arrived
    final = jnp.sum(lax.all_to_all(final, "row", 0, 0, axis_index_groups=QUADS), axis=0)
    pz = final[: 2 * side].reshape(2, side, 2 * width)
    ss = final[2 * side :]
    keep = lax.dynamic_index_in_dim(pz, far, axis=0, keepdims=False)
    give = lax.dynamic_index_in_dim(pz, 1 - far, axis=0, keepdims=False)
    arrived = swap(jnp.concatenate([give, ss], axis=0), 8)
    keep = keep + arrived[:side]
    ss = ss + arrived[side:]
    ss = jnp.where(far == 0, ss[:, :width], ss[:, width:])

    parent_diag = diag_one[0] + keep[:, :width]
    coupled = -(dc_t.T + keep[:, width:])
    child_diag = diag_two[0] + ss
    return (
        -(v_t * mask_one).T[None],
        parent_diag[None],
        (y_t * mask_two).T[None],
        coupled[None],
        child_diag[None],
    )


def solution(mesh):
    placed = (
        P("row", "col"),
        P("branch", None, None),
        P("branch", "row", "col"),
        P("branch", "row", "col"),
        P("branch", "row", "col"),
        P("branch", "row", "col"),
        P("branch", "row", "col"),
    )
    return jax.shard_map(
        body,
        mesh=mesh,
        in_specs=placed,
        out_specs=(P("branch", "row", "col"),) * 5,
        check_vma=False,
    )
```
